32 devices in a mesh: row: 8 (over y, x, core), col: 4 (over z).
Axes of the slice: x: 2, y: 2, z: 4, core: 2. Of those that a mesh axis runs over, the one named last changes fastest.
Arguments:
- tokens: bfloat16 [1024, 16384], P('col', 'row'), may hold values from -160 to 160
- norm_gain: bfloat16 [16384], P('row'), may hold values from 0.5 to 1.5
- gate_weight: bfloat16 [16384, 26624], P('row', 'col'), may hold values from -0.046875 to 0.046875
Outputs:
- gate_out: float32 [1024, 26624], P('row', 'col')
- token_peak: float32 [1024], P('col')
The draws below stay inside these ranges and needn't reach their ends.
All inputs are finite; a program needn't handle non-finite values.
Results may differ from the reference program's by a relative error of at most 0.008.
Values may be sent and summed in bfloat16 or wider, within the bound.
A program may use at most 128 MiB of HBM per device.

```python
import math
import jax
import jax.numpy as jnp
from jax import lax

D = 16384
FFW = 26624
TOKENS = 1024


def draw_tokens(key, part):
    key_base, key_rough, key_rows = jax.random.split(key, 3)
    place = jnp.arange(D, dtype=jnp.float32) / (D - 1)
    rising = 0.6 + 1.2 * place
    rough = jax.random.uniform(key_rough, (D,), jnp.float32, 0.7, 1.4)
    row_scale = jnp.exp(jax.random.uniform(key_rows, (TOKENS, 1), jnp.float32, 0.0, math.log(10.0)))
    base = jnp.clip(jax.random.normal(key_base, (TOKENS, D), jnp.float32), -6.0, 6.0)
    values = base * (rising * rough)[None, :] * row_scale
    return jnp.clip(values, -160.0, 160.0).astype(jnp.bfloat16)


def block_scale(rng, dims, shards, least, top_value):
    loudness = 1.0
    for position, shards_of in shards:
        heights = jax.random.uniform(jax.random.fold_in(jax.random.fold_in(rng, 6), position), (shards_of,), jnp.float32, least / len(shards), top_value / len(shards))
        loudness = loudness * jnp.repeat(jnp.exp(heights), dims[position] // shards_of).reshape((-1,) + (1,) * (len(dims) - 1 - position))
    return loudness


def noise(stream_key, dims, scale, limit, pieces=(), kind=jnp.bfloat16):
    result = scale * jax.random.normal(stream_key, dims, jnp.float32)
    if pieces:
        result = result * block_scale(stream_key, dims, pieces, -0.22, 0.18)
    return jnp.clip(result, -limit, limit).astype(kind)


def setup_inputs(seed: int = 0) -> dict:
    streams_of = jax.random.split(jax.random.key(seed), 4)
    tokens = draw_tokens(jax.random.fold_in(streams_of[3], 71), 0)
    norm_gain = jnp.clip(1.0 + 0.1 * jax.random.normal(streams_of[1], (D,), jnp.float32), 0.5, 1.5).astype(jnp.bfloat16)
    gate_weight = noise(streams_of[2], (D, FFW), D ** -0.5, 0.046875, ((0, 8), (1, 4)))
    return dict(tokens=tokens, norm_gain=norm_gain, gate_weight=gate_weight)


def reference(tokens, norm_gain, gate_weight):
    values = tokens.astype(jnp.float32)
    mean_square = lax.optimization_barrier(jnp.sum(values * values, axis=1)) / D
    inverse = lax.rsqrt(mean_square + 1e-05)
    normed = values * inverse[:, None] * norm_gain.astype(jnp.float32)[None, :]
    token_peak = lax.optimization_barrier(jnp.max(jnp.abs(normed), axis=1))
    scale = ((token_peak + 1e-06) / 448.0).astype(jnp.bfloat16)
    quant = (normed / scale.astype(jnp.float32)[:, None]).astype(jnp.bfloat16)
    product = jnp.dot(quant, gate_weight, preferred_element_type=jnp.float32)
    gate_out = product * scale.astype(jnp.float32)[:, None]
    return (gate_out, token_peak)
```

```python
import functools

import jax
import jax.numpy as jnp
from jax import lax
from jax.experimental import pallas as pl
from jax.experimental.pallas import tpu as pltpu
from jax.sharding import PartitionSpec as P

MESH = pl.DeviceIdType.MESH
D1 = 1
D2 = 2
ROWS = 32


def kernel(R, C, NC, w, B, K, tok_ref, gain_ref, wgt_ref, out_ref, peak_ref,
           wv, x, xg, sq, mx, own, psend, precv, cha, chb, outbuf, fac, stsrc, statc, statb,
           tok_sem, w_sem, zr_send, zl_send, z_recv, psend_sem, precv_sem,
           ca_send, ca_recv, cb_send, cb_recv, out_sem, sc_send, sc_recv, sb_send, sb_recv):
    r = lax.axis_index("row")
    c = lax.axis_index("col")
    n_chips = R // 2
    half_ring = n_chips // 2
    chip = r // 2
    core = r % 2
    partner = r + 1 - 2 * core
    H = B // 2
    Q = H // 2
    items = C * NC
    slots = own.shape[0]

    def ring_pos(i):
        return jnp.where(i % 2 == 0, i // 2, 2 * half_ring - 1 - i // 2)

    def ring_chip(q):
        return jnp.where(q < half_ring, 2 * q, 2 * (2 * half_ring - 1 - q) + 1)

    pos = ring_pos(chip)
    nxt = ring_chip((pos + 1) % n_chips) * 2 + core
    prv = ring_chip((pos + n_chips - 1) % n_chips) * 2 + core

    near = jnp.minimum(c, C - 1 - c)

    def block_of(i):
        step = (i + 1) // 2
        close = jnp.where(i % 2 == 1, c - step, c + step)
        far = jnp.where(c <= C - 1 - c, c + (i - near), c - (i - near))
        return jnp.where(i <= 2 * near, close, far)

    tok_copy = pltpu.make_async_copy(tok_ref, x.at[c], tok_sem)
    tok_copy.start()

    def w_copy(n):
        cols = pl.ds(pl.multiple_of(n * w, w), w)
        return pltpu.make_async_copy(wgt_ref.at[:, cols], wv.at[n], w_sem.at[n])

    barrier = pltpu.get_barrier_semaphore()
    for o in range(1, R):
        pl.semaphore_signal(barrier, inc=1, device_id={"row": (r + o) % R}, device_id_type=MESH)

    @pl.when(c > 0)
    def _():
        pl.semaphore_signal(barrier, inc=1, device_id={"col": c - 1}, device_id_type=MESH)

    @pl.when(c < C - 1)
    def _():
        pl.semaphore_signal(barrier, inc=1, device_id={"col": c + 1}, device_id_type=MESH)

    @pl.loop(0, NC)
    def _(n):
        w_copy(n).start()

    neighbours = jnp.where(c > 0, 1, 0) + jnp.where(c < C - 1, 1, 0)
    pl.semaphore_wait(barrier, R - 1 + neighbours)

    def z_right(src, b, s):
        return pltpu.make_async_remote_copy(
            src_ref=src, dst_ref=x.at[b], send_sem=zr_send.at[s], recv_sem=z_recv.at[b],
            device_id={"col": c + 1}, device_id_type=MESH)

    def z_left(src, b, s):
        return pltpu.make_async_remote_copy(
            src_ref=src, dst_ref=x.at[b], send_sem=zl_send.at[s], recv_sem=z_recv.at[b],
            device_id={"col": c - 1}, device_id_type=MESH)

    @pl.when(c < C - 1)
    def _():
        z_right(tok_ref, c, 0).start()

    @pl.when(c > 0)
    def _():
        z_left(tok_ref, c, 0).start()

    tok_copy.wait()

    def part_copy(g):
        return pltpu.make_async_remote_copy(
            src_ref=psend.at[g], dst_ref=precv.at[g], send_sem=psend_sem.at[g], recv_sem=precv_sem.at[g],
            device_id={"row": partner}, device_id_type=MESH)

    def chain_copy(buf, send, recv, g, to):
        return pltpu.make_async_remote_copy(
            src_ref=buf.at[g], dst_ref=buf.at[g], send_sem=send.at[g], recv_sem=recv.at[g],
            device_id={"row": to}, device_id_type=MESH)

    def statc_copy(o):
        return pltpu.make_async_remote_copy(
            src_ref=stsrc.at[0], dst_ref=statc.at[r], send_sem=sc_send.at[o], recv_sem=sc_recv.at[r],
            device_id={"row": (r + o) % R}, device_id_type=MESH)

    def statb_copy(i, k, to):
        return pltpu.make_async_remote_copy(
            src_ref=stsrc.at[i], dst_ref=statb.at[r], send_sem=sb_send.at[i, k], recv_sem=sb_recv.at[r],
            device_id={"row": to}, device_id_type=MESH)

    def stat_wait(buf, sem, o):
        q = (r + o) % R
        pltpu.make_async_remote_copy(
            src_ref=stsrc.at[0], dst_ref=buf.at[q], send_sem=sc_send.at[0], recv_sem=sem.at[q],
            device_id={"row": q}, device_id_type=MESH).wait_recv()

    def out_copy(h, n):
        rows = pl.ds(h * Q, Q)
        cols = pl.ds(pl.multiple_of(n * w, w), w)
        return pltpu.make_async_copy(outbuf.at[rows, cols], out_ref.at[rows, cols], out_sem.at[h, n])

    def start_block(i):
        b = block_of(i)

        @pl.when((i > 0) & (c - i >= 0))
        def _():
            z_right(x.at[c - i], c - i, 0).wait_recv()

            @pl.when(c < C - 1)
            def _():
                z_right(x.at[c - i], c - i, i).start()

        @pl.when((i > 0) & (c + i <= C - 1))
        def _():
            z_left(x.at[c + i], c + i, 0).wait_recv()

            @pl.when(c > 0)
            def _():
                z_left(x.at[c + i], c + i, i).start()

        gain = gain_ref[...].astype(jnp.float32)

        @pl.loop(0, B // ROWS)
        def _(q):
            rows = pl.ds(pl.multiple_of(q * ROWS, ROWS), ROWS)
            total = jnp.zeros((ROWS, 128), jnp.float32)
            top = jnp.zeros((ROWS, 128), jnp.float32)
            for j in range(K // 128):
                cols = slice(j * 128, (j + 1) * 128)
                v = x[b, rows, cols].astype(jnp.float32)
                y = v * gain[:, cols]
                total = total + v * v
                top = jnp.maximum(top, jnp.abs(y))
                xg[rows, cols] = y.astype(jnp.bfloat16)
            sq[rows, :] = total
            mx[rows, :] = top

        s = jnp.sum(sq[...].T, axis=0, keepdims=True)
        m = jnp.max(mx[...].T, axis=0, keepdims=True)
        line = lax.broadcasted_iota(jnp.int32, (8, B), 0)
        both = jnp.where(line < 4, jnp.broadcast_to(s, (8, B)), jnp.broadcast_to(m, (8, B)))
        stsrc[i] = both

        @pl.when(i == 0)
        def _():
            statc[r] = both
            for o in range(1, R):
                statc_copy(o).start()

        @pl.when(chip == b)
        def _():
            statb[r] = both

        for k in range(2):
            @pl.when(r != 2 * b + k)
            def _():
                statb_copy(i, k, 2 * b + k).start()

    def totals(buf):
        s = buf[0, 0:4, :]
        m = buf[0, 4:8, :]
        for q in range(1, R):
            s = s + buf[q, 0:4, :]
            m = jnp.maximum(m, buf[q, 4:8, :])
        inverse = lax.rsqrt(s / (K * R) + 1e-05)
        return inverse, m * inverse

    def make_factor():
        for o in range(1, R):
            stat_wait(statb, sb_recv, o)
        inverse, peak = totals(statb)
        scale = ((peak + 1e-06) / 448.0).astype(jnp.bfloat16).astype(jnp.float32)
        factor = (inverse / scale) * scale
        mine = jnp.where(core == 0, factor[0:1, :H], factor[0:1, H:])
        fac[...] = jnp.broadcast_to(mine, (H, H)).T

    def chain(g, lag, h, buf, send, recv, to):
        i = g // NC
        n = g % NC
        b_pos = ring_pos(block_of(i))
        stage = (pos + n_chips - b_pos - 1) % n_chips if h == 0 else (b_pos + n_chips - pos - 1) % n_chips

        @pl.when(stage == lag)
        def _():
            rows = slice(h * Q, (h + 1) * Q)
            v = own[g % slots, rows, :]
            if lag > 0:
                chain_copy(buf, send, recv, g, to).wait_recv()
                v = v + buf[g].astype(jnp.float32)
            if lag < n_chips - 1:
                buf[g] = v.astype(jnp.bfloat16)
                chain_copy(buf, send, recv, g, to).start()
            else:
                if h == 0:
                    @pl.when(n == 0)
                    def _():
                        make_factor()
                f = fac[rows, 0:1]
                cols = pl.ds(pl.multiple_of(n * w, w), w)
                outbuf[rows, cols] = v * f
                out_copy(h, n).start()

    @pl.loop(0, items + D1 + (n_chips - 1) * D2)
    def _(t):
        @pl.when(t < items)
        def _():
            i = t // NC
            n = t % NC

            @pl.when(n == 0)
            def _():
                start_block(i)

            @pl.when(i == 0)
            def _():
                w_copy(n).wait()

            product = jnp.dot(xg[...], wv[n], preferred_element_type=jnp.float32)
            own[t % slots] = jnp.where(core == 0, product[:H], product[H:])
            psend[t] = jnp.where(core == 0, product[H:], product[:H]).astype(jnp.bfloat16)
            part_copy(t).start()

        g0 = t - D1

        @pl.when((g0 >= 0) & (g0 < items))
        def _():
            part_copy(g0).wait_recv()
            own[g0 % slots] = own[g0 % slots] + precv[g0].astype(jnp.float32)

        for lag in range(n_chips):
            g = t - D1 - lag * D2

            @pl.when((g >= 0) & (g < items))
            def _():
                chain(g, lag, 0, cha, ca_send, ca_recv, nxt)
                chain(g, lag, 1, chb, cb_send, cb_recv, prv)

    for o in range(1, R):
        stat_wait(statc, sc_recv, o)
    _, peak = totals(statc)
    peak_ref[...] = peak[0:1, :]

    @pl.loop(0, items)
    def _(g):
        part_copy(g).wait_send()
        mine = block_of(g // NC) == chip

        @pl.when(jnp.logical_not(mine))
        def _():
            chain_copy(cha, ca_send, ca_recv, g, nxt).wait_send()
            chain_copy(chb, cb_send, cb_recv, g, prv).wait_send()

    for s in range(C - 1):
        @pl.when((c < C - 1) & (c - s >= 0))
        def _():
            z_right(tok_ref, c, s).wait_send()

        @pl.when((c > 0) & (c + s <= C - 1))
        def _():
            z_left(tok_ref, c, s).wait_send()

    for o in range(1, R):
        statc_copy(o).wait_send()
    for i in range(C):
        b = block_of(i)
        for k in range(2):
            @pl.when(r != 2 * b + k)
            def _():
                statb_copy(i, k, 2 * b + k).wait_send()

    @pl.loop(0, NC)
    def _(n):
        out_copy(0, n).wait()
        out_copy(1, n).wait()


def shards(R, C, tokens, norm_gain, gate_weight):
    B, K = tokens.shape
    F = gate_weight.shape[1]
    w = max(v for v in range(128, 513, 128) if F % v == 0)
    NC = F // w
    H = B // 2
    n_chips = R // 2
    assert R == 2 * C and n_chips % 2 == 0
    items = C * NC
    slots = D1 + (n_chips - 1) * D2 + 1
    dma = pltpu.SemaphoreType.DMA
    out, peak = pl.pallas_call(
        functools.partial(kernel, R, C, NC, w, B, K),
        out_shape=(
            jax.ShapeDtypeStruct((H, F), jnp.float32),
            jax.ShapeDtypeStruct((1, B), jnp.float32),
        ),
        in_specs=[
            pl.BlockSpec(memory_space=pl.ANY),
            pl.BlockSpec(memory_space=pltpu.VMEM),
            pl.BlockSpec(memory_space=pl.ANY),
        ],
        out_specs=(
            pl.BlockSpec(memory_space=pl.ANY),
            pl.BlockSpec(memory_space=pltpu.VMEM),
        ),
        scratch_shapes=[
            pltpu.VMEM((NC, K, w), jnp.bfloat16),
            pltpu.VMEM((C, B, K), jnp.bfloat16),
            pltpu.VMEM((B, K), jnp.bfloat16),
            pltpu.VMEM((B, 128), jnp.float32),
            pltpu.VMEM((B, 128), jnp.float32),
            pltpu.VMEM((slots, H, w), jnp.float32),
            pltpu.VMEM((items, H, w), jnp.bfloat16),
            pltpu.VMEM((items, H, w), jnp.bfloat16),
            pltpu.VMEM((items, H // 2, w), jnp.bfloat16),
            pltpu.VMEM((items, H // 2, w), jnp.bfloat16),
            pltpu.VMEM((H, F), jnp.float32),
            pltpu.VMEM((H, H), jnp.float32),
            pltpu.VMEM((C, 8, B), jnp.float32),
            pltpu.VMEM((R, 8, B), jnp.float32),
            pltpu.VMEM((R, 8, B), jnp.float32),
            dma,
            dma((NC,)),
            dma((C,)),
            dma((C,)),
            dma((C,)),
            dma((items,)),
            dma((items,)),
            dma((items,)),
            dma((items,)),
            dma((items,)),
            dma((items,)),
            dma((2, NC)),
            dma((R,)),
            dma((R,)),
            dma((C, 2)),
            dma((R,)),
        ],
        compiler_params=pltpu.CompilerParams(
            collective_id=0, has_side_effects=True, vmem_limit_bytes=67043328
        ),
    )(tokens, norm_gain.reshape(1, K), gate_weight)
    return out, peak.reshape(B)


def solution(mesh):
    in_specs = (P("col", "row"), P("row"), P("row", "col"))
    out_specs = (P("row", "col"), P("col"))
    f = functools.partial(shards, mesh.shape["row"], mesh.shape["col"])
    return jax.shard_map(f, mesh=mesh, in_specs=in_specs, out_specs=out_specs, check_vma=False)
```

```python
import functools

import jax
import jax.numpy as jnp
from jax import lax
from jax.experimental import pallas as pl
from jax.experimental.pallas import tpu as pltpu
from jax.sharding import PartitionSpec as P

MESH = pl.DeviceIdType.MESH
D1 = 1
D2 = 3
ROWS = 32


def lag_step(NC, n_chips):
    return min(D2, (NC - D1) // (n_chips - 1))


def kernel(R, C, NC, w, B, K, tok_ref, gain_ref, wgt_ref, out_ref, peak_ref,
           wv, x, xg, sq, mx, own, psend, precv, cha, chb, outbuf, fac, stsrc, statc, statb,
           tok_sem, w_sem, zr_send, zl_send, z_recv, psend_sem, precv_sem,
           ca_send, ca_recv, cb_send, cb_recv, out_sem, sc_send, sc_recv, sb_send, sb_recv):
    r = lax.axis_index("row")
    c = lax.axis_index("col")
    n_chips = R // 2
    half_ring = n_chips // 2
    chip = r // 2
    core = r % 2
    partner = r + 1 - 2 * core
    H = B // 2
    Q = H // 2
    items = C * NC
    slots = own.shape[0]
    d2 = lag_step(NC, n_chips)
    last = D1 + (n_chips - 1) * d2

    def ring_pos(i):
        return jnp.where(i % 2 == 0, i // 2, 2 * half_ring - 1 - i // 2)

    def ring_chip(q):
        return jnp.where(q < half_ring, 2 * q, 2 * (2 * half_ring - 1 - q) + 1)

    pos = ring_pos(chip)
    nxt = ring_chip((pos + 1) % n_chips) * 2 + core
    prv = ring_chip((pos + n_chips - 1) % n_chips) * 2 + core

    near = jnp.minimum(c, C - 1 - c)

    def block_of(i):
        step = (i + 1) // 2
        close = jnp.where(i % 2 == 1, c - step, c + step)
        far = jnp.where(c <= C - 1 - c, c + (i - near), c - (i - near))
        return jnp.where(i <= 2 * near, close, far)

    tok_copy = pltpu.make_async_copy(tok_ref, x.at[c], tok_sem)
    tok_copy.start()

    def w_copy(n):
        cols = pl.ds(pl.multiple_of(n * w, w), w)
        return pltpu.make_async_copy(wgt_ref.at[:, cols], wv.at[n], w_sem.at[n])

    barrier = pltpu.get_barrier_semaphore()
    for o in range(1, R):
        pl.semaphore_signal(barrier, inc=1, device_id={"row": (r + o) % R}, device_id_type=MESH)

    @pl.when(c > 0)
    def _():
        pl.semaphore_signal(barrier, inc=1, device_id={"col": c - 1}, device_id_type=MESH)

    @pl.when(c < C - 1)
    def _():
        pl.semaphore_signal(barrier, inc=1, device_id={"col": c + 1}, device_id_type=MESH)

    @pl.loop(0, NC)
    def _(n):
        w_copy(n).start()

    neighbours = jnp.where(c > 0, 1, 0) + jnp.where(c < C - 1, 1, 0)
    pl.semaphore_wait(barrier, R - 1 + neighbours)

    def z_right(src, b, s):
        return pltpu.make_async_remote_copy(
            src_ref=src, dst_ref=x.at[b], send_sem=zr_send.at[s], recv_sem=z_recv.at[b],
            device_id={"col": c + 1}, device_id_type=MESH)

    def z_left(src, b, s):
        return pltpu.make_async_remote_copy(
            src_ref=src, dst_ref=x.at[b], send_sem=zl_send.at[s], recv_sem=z_recv.at[b],
            device_id={"col": c - 1}, device_id_type=MESH)

    @pl.when(c < C - 1)
    def _():
        z_right(tok_ref, c, 0).start()

    @pl.when(c > 0)
    def _():
        z_left(tok_ref, c, 0).start()

    tok_copy.wait()

    def part_copy(g):
        return pltpu.make_async_remote_copy(
            src_ref=psend.at[g], dst_ref=precv.at[g], send_sem=psend_sem.at[g], recv_sem=precv_sem.at[g],
            device_id={"row": partner}, device_id_type=MESH)

    def chain_copy(buf, send, recv, g, to):
        return pltpu.make_async_remote_copy(
            src_ref=buf.at[g], dst_ref=buf.at[g], send_sem=send.at[g], recv_sem=recv.at[g],
            device_id={"row": to}, device_id_type=MESH)

    def statc_copy(o):
        return pltpu.make_async_remote_copy(
            src_ref=stsrc.at[0], dst_ref=statc.at[r], send_sem=sc_send.at[o], recv_sem=sc_recv.at[r],
            device_id={"row": (r + o) % R}, device_id_type=MESH)

    def statb_copy(i, k, to):
        return pltpu.make_async_remote_copy(
            src_ref=stsrc.at[i], dst_ref=statb.at[r], send_sem=sb_send.at[i, k], recv_sem=sb_recv.at[r],
            device_id={"row": to}, device_id_type=MESH)

    def stat_wait(buf, sem, o):
        q = (r + o) % R
        pltpu.make_async_remote_copy(
            src_ref=stsrc.at[0], dst_ref=buf.at[q], send_sem=sc_send.at[0], recv_sem=sem.at[q],
            device_id={"row": q}, device_id_type=MESH).wait_recv()

    def out_copy(h, n):
        rows = pl.ds(h * Q, Q)
        cols = pl.ds(pl.multiple_of(n * w, w), w)
        return pltpu.make_async_copy(outbuf.at[rows, cols], out_ref.at[rows, cols], out_sem.at[h, n])

    def start_block(i):
        b = block_of(i)

        @pl.when((i > 0) & (c - i >= 0))
        def _():
            z_right(x.at[c - i], c - i, 0).wait_recv()

            @pl.when(c < C - 1)
            def _():
                z_right(x.at[c - i], c - i, i).start()

        @pl.when((i > 0) & (c + i <= C - 1))
        def _():
            z_left(x.at[c + i], c + i, 0).wait_recv()

            @pl.when(c > 0)
            def _():
                z_left(x.at[c + i], c + i, i).start()

        gain = gain_ref[...].astype(jnp.float32)

        @pl.loop(0, B // ROWS)
        def _(q):
            rows = pl.ds(pl.multiple_of(q * ROWS, ROWS), ROWS)
            total = jnp.zeros((ROWS, 128), jnp.float32)
            top = jnp.zeros((ROWS, 128), jnp.float32)
            for j in range(K // 128):
                cols = slice(j * 128, (j + 1) * 128)
                v = x[b, rows, cols].astype(jnp.float32)
                y = v * gain[:, cols]
                total = total + v * v
                top = jnp.maximum(top, jnp.abs(y))
                xg[rows, cols] = y.astype(jnp.bfloat16)
            sq[rows, :] = total
            mx[rows, :] = top

        s = jnp.sum(sq[...].T, axis=0, keepdims=True)
        m = jnp.max(mx[...].T, axis=0, keepdims=True)
        line = lax.broadcasted_iota(jnp.int32, (8, B), 0)
        both = jnp.where(line < 4, jnp.broadcast_to(s, (8, B)), jnp.broadcast_to(m, (8, B)))
        stsrc[i] = both

        @pl.when(i == 0)
        def _():
            statc[r] = both
            for o in range(1, R):
                statc_copy(o).start()

        @pl.when(chip == b)
        def _():
            statb[r] = both

        for k in range(2):
            @pl.when(r != 2 * b + k)
            def _():
                statb_copy(i, k, 2 * b + k).start()

    def totals(buf):
        s = buf[0, 0:4, :]
        m = buf[0, 4:8, :]
        for q in range(1, R):
            s = s + buf[q, 0:4, :]
            m = jnp.maximum(m, buf[q, 4:8, :])
        inverse = lax.rsqrt(s / (K * R) + 1e-05)
        return inverse, m * inverse

    def make_factor():
        for o in range(1, R):
            stat_wait(statb, sb_recv, o)
        inverse, peak = totals(statb)
        scale = ((peak + 1e-06) / 448.0).astype(jnp.bfloat16).astype(jnp.float32)
        factor = (inverse / scale) * scale
        mine = jnp.where(core == 0, factor[0:1, :H], factor[0:1, H:])
        fac[...] = jnp.broadcast_to(mine, (H, H)).T

    def chain(stage, g, n, slot, lag, h, buf, send, recv, to):
        @pl.when(stage == lag)
        def _():
            rows = slice(h * Q, (h + 1) * Q)
            v = own[slot, rows, :]
            if lag > 0:
                chain_copy(buf, send, recv, g, to).wait_recv()
                v = v + buf[g].astype(jnp.float32)
            if lag < n_chips - 1:
                buf[g] = v.astype(jnp.bfloat16)
                chain_copy(buf, send, recv, g, to).start()
            else:
                if h == 0:
                    @pl.when(n == 0)
                    def _():
                        make_factor()
                f = fac[rows, 0:1]
                cols = pl.ds(pl.multiple_of(n * w, w), w)
                outbuf[rows, cols] = v * f
                out_copy(h, n).start()

    def stages(i):
        ahead = pos + n_chips - ring_pos(block_of(i)) - 1
        after = 2 * n_chips - 2 - ahead
        wrap = lambda v: jnp.where(v >= n_chips, v - n_chips, v)
        return wrap(ahead), wrap(after)

    @pl.loop(0, C + 1)
    def _(i):
        live = i < C
        now_a, now_b = stages(jnp.minimum(i, C - 1))
        old_a, old_b = stages(jnp.maximum(i - 1, 0))
        now_a = jnp.where(live, now_a, -1)
        now_b = jnp.where(live, now_b, -1)
        old_a = jnp.where(i > 0, old_a, -1)
        old_b = jnp.where(i > 0, old_b, -1)
        base = i * NC

        @pl.when(live)
        def _():
            start_block(i)

        @pl.loop(0, jnp.where(live, NC, last))
        def _(n):
            t = base + n

            @pl.when(live)
            def _():
                @pl.when(i == 0)
                def _():
                    w_copy(n).wait()

                slot = lax.rem(t, slots)
                product = jnp.dot(xg[...], wv[n], preferred_element_type=jnp.float32)
                own[slot] = jnp.where(core == 0, product[:H], product[H:])
                psend[t] = jnp.where(core == 0, product[H:], product[:H]).astype(jnp.bfloat16)
                part_copy(t).start()

            g0 = t - D1

            @pl.when((g0 >= 0) & (g0 < items))
            def _():
                part_copy(g0).wait_recv()
                slot = lax.rem(g0, slots)
                own[slot] = own[slot] + precv[g0].astype(jnp.float32)

            for lag in range(n_chips):
                off = D1 + lag * d2
                fresh = n >= off
                g = jnp.maximum(t - off, 0)
                m = jnp.where(fresh, n - off, n - off + NC)
                slot = lax.rem(g, slots)
                chain(jnp.where(fresh, now_a, old_a), g, m, slot, lag, 0, cha, ca_send, ca_recv, nxt)
                chain(jnp.where(fresh, now_b, old_b), g, m, slot, lag, 1, chb, cb_send, cb_recv, prv)

    for o in range(1, R):
        stat_wait(statc, sc_recv, o)
    _, peak = totals(statc)
    peak_ref[...] = peak[0:1, :]

    @pl.loop(0, items)
    def _(g):
        part_copy(g).wait_send()
        mine = block_of(g // NC) == chip

        @pl.when(jnp.logical_not(mine))
        def _():
            chain_copy(cha, ca_send, ca_recv, g, nxt).wait_send()
            chain_copy(chb, cb_send, cb_recv, g, prv).wait_send()

    for s in range(C - 1):
        @pl.when((c < C - 1) & (c - s >= 0))
        def _():
            z_right(tok_ref, c, s).wait_send()

        @pl.when((c > 0) & (c + s <= C - 1))
        def _():
            z_left(tok_ref, c, s).wait_send()

    for o in range(1, R):
        statc_copy(o).wait_send()
    for i in range(C):
        b = block_of(i)
        for k in range(2):
            @pl.when(r != 2 * b + k)
            def _():
                statb_copy(i, k, 2 * b + k).wait_send()

    @pl.loop(0, NC)
    def _(n):
        out_copy(0, n).wait()
        out_copy(1, n).wait()


def shards(R, C, tokens, norm_gain, gate_weight):
    B, K = tokens.shape
    F = gate_weight.shape[1]
    w = max(v for v in range(128, 513, 128) if F % v == 0)
    NC = F // w
    H = B // 2
    n_chips = R // 2
    assert R == 2 * C and n_chips % 2 == 0
    items = C * NC
    slots = 1
    while slots < D1 + (n_chips - 1) * lag_step(NC, n_chips) + 1:
        slots *= 2
    dma = pltpu.SemaphoreType.DMA
    out, peak = pl.pallas_call(
        functools.partial(kernel, R, C, NC, w, B, K),
        out_shape=(
            jax.ShapeDtypeStruct((H, F), jnp.float32),
            jax.ShapeDtypeStruct((1, B), jnp.float32),
        ),
        in_specs=[
            pl.BlockSpec(memory_space=pl.ANY),
            pl.BlockSpec(memory_space=pltpu.VMEM),
            pl.BlockSpec(memory_space=pl.ANY),
        ],
        out_specs=(
            pl.BlockSpec(memory_space=pl.ANY),
            pl.BlockSpec(memory_space=pltpu.VMEM),
        ),
        scratch_shapes=[
            pltpu.VMEM((NC, K, w), jnp.bfloat16),
            pltpu.VMEM((C, B, K), jnp.bfloat16),
            pltpu.VMEM((B, K), jnp.bfloat16),
            pltpu.VMEM((B, 128), jnp.float32),
            pltpu.VMEM((B, 128), jnp.float32),
            pltpu.VMEM((slots, H, w), jnp.float32),
            pltpu.VMEM((items, H, w), jnp.bfloat16),
            pltpu.VMEM((items, H, w), jnp.bfloat16),
            pltpu.VMEM((items, H // 2, w), jnp.bfloat16),
            pltpu.VMEM((items, H // 2, w), jnp.bfloat16),
            pltpu.VMEM((H, F), jnp.float32),
            pltpu.VMEM((H, H), jnp.float32),
            pltpu.VMEM((C, 8, B), jnp.float32),
            pltpu.VMEM((R, 8, B), jnp.float32),
            pltpu.VMEM((R, 8, B), jnp.float32),
            dma,
            dma((NC,)),
            dma((C,)),
            dma((C,)),
            dma((C,)),
            dma((items,)),
            dma((items,)),
            dma((items,)),
            dma((items,)),
            dma((items,)),
            dma((items,)),
            dma((2, NC)),
            dma((R,)),
            dma((R,)),
            dma((C, 2)),
            dma((R,)),
        ],
        compiler_params=pltpu.CompilerParams(
            collective_id=0, has_side_effects=True, vmem_limit_bytes=67043328
        ),
    )(tokens, norm_gain.reshape(1, K), gate_weight)
    return out, peak.reshape(B)


def solution(mesh):
    in_specs = (P("col", "row"), P("row"), P("row", "col"))
    out_specs = (P("row", "col"), P("col"))
    f = functools.partial(shards, mesh.shape["row"], mesh.shape["col"])
    return jax.shard_map(f, mesh=mesh, in_specs=in_specs, out_specs=out_specs, check_vma=False)
```
